512 devices in a mesh: gx: 32 (over x, z_hi, core), gy: 16 (over z_lo, y).
Axes of the slice: x: 4, y: 8, z: 8 (z_hi: 4, z_lo: 2; z = z_hi * 2 + z_lo), core: 2. Of those that a mesh axis runs over, the one named last changes fastest.
Arguments:
- coefficients: float32 [32, 16, 256, 1024], P('gx', 'gy'), may hold values from -6 to 6
- transfer_blocks: float32 [4, 32, 16, 256, 512], P(None, 'gx', 'gy'), may hold values from -0.25 to 0.25
Outputs:
- result_blocks: float32 [32, 16, 256, 1024], P('gx', 'gy')
The draws below stay inside these ranges and needn't reach their ends.
All inputs are finite; a program needn't handle non-finite values.
Results may differ from the reference program's by a relative error of at most 0.0001.
Values sent between devices are 32-bit elements; how exact they have to be, the bound alone decides.
No kernel may reach another device: no remote copies, remote signals or barrier semaphores. Data moves between devices by JAX's collectives and lax.ppermute only.
A program may use at most 64 MiB of HBM per device.

```python
import jax
import jax.numpy as jnp
from jax import lax

RANK = 256
NRHS = 1024
LEVELS = 4
BX = 32
BY = 16


def block_levels(rng, shape, split, smallest, high):
    gain = 1.0
    for axis_at, shards_of in split:
        steps = jax.random.uniform(jax.random.fold_in(jax.random.fold_in(rng, 6), axis_at), (shards_of,), jnp.float32, smallest / len(split), high / len(split))
        gain = gain * jnp.repeat(jnp.exp(steps), shape[axis_at] // shards_of).reshape((-1,) + (1,) * (len(shape) - 1 - axis_at))
    return gain


def gaussian(stream_key, shape, deviation, reach, cuts=(), kind=jnp.bfloat16):
    level = block_levels(stream_key, shape, cuts, -0.22, 0.18) if cuts else 1.0
    result = jax.random.normal(stream_key, shape, jnp.float32) * deviation * level
    return jnp.minimum(jnp.maximum(result, -reach), reach).astype(kind)


def setup_inputs(seed: int = 0) -> dict:
    streams_of = jax.random.split(jax.random.key(seed), 3)
    coefficients = gaussian(streams_of[0], (BX, BY, RANK, NRHS), 1.0, 6.0, ((0, 32), (1, 16)), jnp.float32)
    transfer_blocks = gaussian(streams_of[1], (LEVELS, BX, BY, RANK, 2 * RANK), (2 * RANK) ** -0.5, 0.25, ((1, 32), (2, 16)), jnp.float32)
    return dict(coefficients=coefficients, transfer_blocks=transfer_blocks)


def apply_level(state, blocks, axis_number, bit_number):
    block_count = state.shape[axis_number]
    position = jnp.arange(block_count, dtype=jnp.int32)
    partner = jnp.take(state, jnp.bitwise_xor(position, jnp.int32(1 << bit_number)), axis=axis_number)
    upper_bit = jnp.bitwise_and(jnp.right_shift(position, bit_number), 1)
    if axis_number == 0:
        upper_bit = upper_bit.reshape(-1, 1, 1, 1)
    else:
        upper_bit = upper_bit.reshape(1, -1, 1, 1)
    lower_block = jnp.where(upper_bit == 0, state, partner)
    upper_block = jnp.where(upper_bit == 0, partner, state)
    first_term = jnp.einsum("xyrk,xykn->xyrn", blocks[..., :RANK], lower_block, precision=lax.Precision.HIGHEST)
    second_term = jnp.einsum("xyrk,xykn->xyrn", blocks[..., RANK:], upper_block, precision=lax.Precision.HIGHEST)
    return first_term + second_term


def reference(coefficients, transfer_blocks):
    high_top = BX.bit_length() - 2
    low_top = BY.bit_length() - 2
    plan = [(0, high_top), (1, low_top), (0, high_top - 1), (1, low_top - 1)]
    state = coefficients
    for level_number in range(LEVELS):
        axis_number, bit_number = plan[level_number]
        state = apply_level(state, transfer_blocks[level_number], axis_number, bit_number)
    return state
```

```python
import jax
import jax.numpy as jnp
from jax import lax
from jax.sharding import PartitionSpec as P


WIDTHS = (2, 3, 3)
ORDER = ((0, 0), (0, 1), (0, 2), (1, 0), (1, 1), (2, 0), (1, 2), (2, 1), (3, 0), (3, 1), (2, 2), (3, 2))


def plan():
    high_top = lax.axis_size("gx").bit_length() - 2
    low_top = lax.axis_size("gy").bit_length() - 2
    return [("gx", high_top), ("gy", low_top), ("gx", high_top - 1), ("gy", low_top - 1)]


def exchange(block, axis, bit):
    route = [(i, i ^ (1 << bit)) for i in range(lax.axis_size(axis))]
    return lax.ppermute(block, axis, route)


def dot(left, right):
    return jnp.dot(left, right, preferred_element_type=jnp.float32, precision=lax.Precision.HIGH)


def on_device(coefficients, transfer_blocks):
    state = coefficients[0, 0]
    rank, columns = state.shape
    edges = [0]
    for width in WIDTHS:
        edges.append(edges[-1] + width * (columns // 8))
    levels = plan()
    halves = []
    for level, (axis, bit) in enumerate(levels):
        block = transfer_blocks[level, 0, 0]
        upper = jnp.bitwise_and(jnp.right_shift(lax.axis_index(axis), bit), 1)
        mine = lax.dynamic_slice(block, (0, upper * rank), (rank, rank))
        other = lax.dynamic_slice(block, (0, (1 - upper) * rank), (rank, rank))
        halves.append((mine, other))
    pieces = [state[:, a:b] for a, b in zip(edges, edges[1:])]
    for level, piece in ORDER:
        axis, bit = levels[level]
        mine, other = halves[level]
        here = pieces[piece]
        there = exchange(here, axis, bit)
        pieces[piece] = dot(mine, here) + dot(other, there)
    return jnp.concatenate(pieces, axis=1).reshape(coefficients.shape)


def solution(mesh):
    in_specs = (P("gx", "gy", None, None), P(None, "gx", "gy", None, None))
    out_specs = P("gx", "gy", None, None)
    return jax.shard_map(
        on_device, mesh=mesh, in_specs=in_specs, out_specs=out_specs, check_vma=False
    )
```

```python
import functools

import jax
import jax.numpy as jnp
from jax import lax
from jax.experimental import pallas as pl
from jax.experimental.pallas import tpu as pltpu
from jax.sharding import PartitionSpec as P


WIDTHS = (2, 2, 3, 1)
ORDER = (
    ("s", 0, 0), ("o", 0, 0), ("s", 0, 1), ("d", 0, 0),
    ("s", 1, 0), ("o", 1, 0), ("s", 0, 2), ("o", 0, 1),
    ("d", 0, 1), ("s", 1, 1), ("o", 1, 1), ("d", 1, 0),
    ("s", 2, 0), ("o", 2, 0), ("o", 0, 2), ("d", 0, 2),
    ("s", 1, 2), ("o", 1, 2), ("d", 1, 1), ("s", 2, 1),
    ("o", 2, 1), ("d", 2, 0), ("s", 3, 0), ("o", 3, 0),
    ("d", 1, 2), ("s", 2, 2), ("o", 2, 2), ("d", 2, 1),
    ("s", 3, 1), ("o", 3, 1), ("s", 0, 3), ("o", 0, 3),
    ("d", 2, 2), ("s", 3, 2), ("o", 3, 2), ("d", 0, 3),
    ("s", 1, 3), ("o", 1, 3), ("d", 1, 3), ("s", 2, 3),
    ("o", 2, 3), ("d", 2, 3), ("s", 3, 3), ("o", 3, 3),
    ("d", 3, 0), ("d", 3, 1), ("d", 3, 2), ("d", 3, 3),
)
LAST = 3

ANY = pl.BlockSpec(memory_space=pl.ANY)
VMEM = pl.BlockSpec(memory_space=pltpu.VMEM)


def plan():
    high_top = lax.axis_size("gx").bit_length() - 2
    low_top = lax.axis_size("gy").bit_length() - 2
    return [("gx", high_top), ("gy", low_top), ("gx", high_top - 1), ("gy", low_top - 1)]


def exchange(block, axis, bit):
    route = [(i, i ^ (1 << bit)) for i in range(lax.axis_size(axis))]
    return lax.ppermute(block, axis, route)


def parts(value):
    high = value.astype(jnp.bfloat16)
    return high, (value - high.astype(jnp.float32)).astype(jnp.bfloat16)


def dot(left, right):
    single = functools.partial(jnp.dot, preferred_element_type=jnp.float32)
    left_high, left_low = parts(left)
    right_high, right_low = parts(right)
    return (single(left_low, right_high) + single(left_high, right_low)) + single(left_high, right_high)


def call(kernel, **options):
    params = pltpu.CompilerParams(vmem_limit_bytes=4 << 20)
    return pl.pallas_call(kernel, compiler_params=params, **options)


def cost(shape):
    rank, width = shape
    return pl.CostEstimate(
        flops=6 * rank * rank * width, bytes_accessed=8 * rank * width, transcendentals=0
    )


def half(blocks_ref, level, mine, rank):
    axis, bit = plan()[level]
    upper = jnp.bitwise_and(jnp.right_shift(lax.axis_index(axis), bit), 1)
    start = pl.multiple_of((upper if mine else 1 - upper) * rank, rank)
    return blocks_ref[level, 0, 0, :, pl.ds(start, rank)]


def own_product(level, blocks, here):
    rank = here.shape[0]

    def kernel(blocks_ref, here_ref, out_ref):
        out_ref[...] = dot(half(blocks_ref, level, True, rank), here_ref[...])

    return call(
        kernel,
        out_shape=jax.ShapeDtypeStruct(here.shape, here.dtype),
        in_specs=[VMEM, VMEM],
        out_specs=VMEM,
        cost_estimate=cost(here.shape),
        name="own",
    )(blocks, here)


def add_product(level, blocks, there, own):
    rank = there.shape[0]

    def kernel(blocks_ref, there_ref, own_ref, out_ref):
        block = half(blocks_ref, level, False, rank)
        out_ref[...] = own_ref[...] + dot(block, there_ref[...])

    return call(
        kernel,
        out_shape=jax.ShapeDtypeStruct(there.shape, there.dtype),
        in_specs=[VMEM, VMEM, VMEM],
        out_specs=VMEM,
        cost_estimate=cost(there.shape),
        name="add",
    )(blocks, there, own)


def add_in_place(level, blocks, there, own, whole, span, shape):
    rank = there.shape[0]
    a, b = span

    def kernel(blocks_ref, there_ref, own_ref, *refs):
        out_ref, sum_ref, sem = refs[-3:]
        block = half(blocks_ref, level, False, rank)
        sum_ref[...] = own_ref[...] + dot(block, there_ref[...])
        copy = pltpu.make_async_copy(sum_ref, out_ref.at[0, 0, :, a:b], sem)
        copy.start()
        copy.wait()

    operands = [blocks, there, own] + ([] if whole is None else [whole])
    return call(
        kernel,
        out_shape=jax.ShapeDtypeStruct(shape, there.dtype),
        in_specs=[VMEM, VMEM, VMEM, ANY][: len(operands)],
        out_specs=ANY,
        input_output_aliases={} if whole is None else {3: 0},
        scratch_shapes=[pltpu.VMEM(there.shape, there.dtype), pltpu.SemaphoreType.DMA],
        cost_estimate=cost(there.shape),
        name="finish",
    )(*operands)


def split(state, spans):
    def kernel(source, *refs):
        outs, sems = refs[:-1], refs[-1]
        copies = [
            pltpu.make_async_copy(source.at[:, a:b], out, sems.at[i])
            for i, ((a, b), out) in enumerate(zip(spans, outs))
        ]
        for copy in copies:
            copy.start()
        for copy in copies:
            copy.wait()

    return pl.pallas_call(
        kernel,
        out_shape=[jax.ShapeDtypeStruct((state.shape[0], b - a), state.dtype) for a, b in spans],
        compiler_params=pltpu.CompilerParams(vmem_limit_bytes=4 << 20),
        in_specs=[ANY],
        out_specs=[ANY] * len(spans),
        scratch_shapes=[pltpu.SemaphoreType.DMA((len(spans),))],
        name="split",
    )(state)


def on_device(coefficients, transfer_blocks):
    state = coefficients[0, 0]
    columns = state.shape[1]
    edges = [0]
    for width in WIDTHS:
        edges.append(edges[-1] + width * (columns // 8))
    spans = list(zip(edges, edges[1:]))
    levels = plan()
    pieces = list(split(state, spans))
    arrived, owns = {}, {}
    result = None
    for what, level, piece in ORDER:
        if what == "s":
            arrived[level, piece] = exchange(pieces[piece], *levels[level])
            continue
        if what == "o":
            owns[level, piece] = own_product(level, transfer_blocks, pieces[piece])
            continue
        there, own = arrived[level, piece], owns[level, piece]
        if level < LAST:
            pieces[piece] = add_product(level, transfer_blocks, there, own)
        else:
            result = add_in_place(
                level, transfer_blocks, there, own, result, spans[piece], coefficients.shape
            )
    return result


def solution(mesh):
    in_specs = (P("gx", "gy", None, None), P(None, "gx", "gy", None, None))
    out_specs = P("gx", "gy", None, None)
    return jax.shard_map(
        on_device, mesh=mesh, in_specs=in_specs, out_specs=out_specs, check_vma=False
    )
```

```python
import functools

import jax
import jax.numpy as jnp
from jax import lax
from jax.experimental import pallas as pl
from jax.experimental.pallas import tpu as pltpu
from jax.sharding import PartitionSpec as P


BEGINS = ((0, 2, 4), (0, 2, 4), (0, 2, 4, 6), (0, 2, 4, 6))
ORDER = (
    ("s", 0, 0), ("s", 0, 2), ("s", 0, 4), ("d", 0, 0),
    ("s", 1, 0), ("d", 0, 2), ("s", 1, 2), ("d", 1, 0),
    ("s", 2, 0), ("d", 0, 4), ("s", 1, 4), ("d", 1, 2),
    ("s", 2, 2), ("d", 2, 0), ("s", 3, 0), ("d", 2, 2),
    ("s", 3, 2), ("d", 1, 4), ("s", 2, 4), ("s", 2, 6),
    ("d", 2, 4), ("s", 3, 4), ("d", 2, 6), ("s", 3, 6),
    ("d", 3, 0), ("d", 3, 2), ("d", 3, 4), ("d", 3, 6),
)
LAST = 3
EARLY = ()

ANY = pl.BlockSpec(memory_space=pl.ANY)
VMEM = pl.BlockSpec(memory_space=pltpu.VMEM)


def plan():
    high_top = lax.axis_size("gx").bit_length() - 2
    low_top = lax.axis_size("gy").bit_length() - 2
    return [("gx", high_top), ("gy", low_top), ("gx", high_top - 1), ("gy", low_top - 1)]


def exchange(block, axis, bit):
    route = [(i, i ^ (1 << bit)) for i in range(lax.axis_size(axis))]
    return lax.ppermute(block, axis, route)


def parts(value):
    high = value.astype(jnp.bfloat16)
    return high, (value - high.astype(jnp.float32)).astype(jnp.bfloat16)


def dot(left, right):
    single = functools.partial(jnp.dot, preferred_element_type=jnp.float32)
    left_high, left_low = parts(left)
    right_high, right_low = parts(right)
    return (single(left_low, right_high) + single(left_high, right_low)) + single(left_high, right_high)


def call(kernel, limit=4 << 20, **options):
    params = pltpu.CompilerParams(vmem_limit_bytes=limit)
    return pl.pallas_call(kernel, compiler_params=params, **options)


def cost(shape):
    rank, width = shape
    return pl.CostEstimate(
        flops=12 * rank * rank * width, bytes_accessed=12 * rank * width, transcendentals=0
    )


def products(level, blocks_ref, here, there):
    axis, bit = plan()[level]
    rank = here.shape[0]
    upper = jnp.bitwise_and(jnp.right_shift(lax.axis_index(axis), bit), 1)
    mine = blocks_ref[:, pl.ds(pl.multiple_of(upper * rank, rank), rank)]
    other = blocks_ref[:, pl.ds(pl.multiple_of((1 - upper) * rank, rank), rank)]
    return dot(mine, here) + dot(other, there)


def fetch(level, blocks_ref, held_ref, sem):
    copy = pltpu.make_async_copy(blocks_ref.at[level, 0, 0], held_ref, sem)
    copy.start()
    copy.wait()


def held(blocks):
    return [pltpu.VMEM(blocks.shape[3:], blocks.dtype), pltpu.SemaphoreType.DMA]


def apply(level, blocks, here, there, spans, limit):
    rank = here.shape[0]

    def kernel(blocks_ref, here_ref, there_ref, *refs):
        *outs, held_ref, sem = refs
        fetch(level, blocks_ref, held_ref, sem)
        for (a, b), out in zip(spans, outs):
            out[...] = products(level, held_ref, here_ref[:, a:b], there_ref[:, a:b])

    return call(
        kernel,
        out_shape=[jax.ShapeDtypeStruct((rank, b - a), here.dtype) for a, b in spans],
        in_specs=[ANY, VMEM, VMEM],
        out_specs=[VMEM] * len(spans),
        scratch_shapes=held(blocks),
        cost_estimate=cost(here.shape),
        limit=limit,
        name="apply",
    )(blocks, here, there)


def apply_in_place(level, blocks, here, there, whole, span, shape):
    a, b = span

    def kernel(blocks_ref, here_ref, there_ref, *refs):
        out_ref, sum_ref, held_ref, sem = refs[-4:]
        fetch(level, blocks_ref, held_ref, sem)
        sum_ref[...] = products(level, held_ref, here_ref[...], there_ref[...])
        copy = pltpu.make_async_copy(sum_ref, out_ref.at[0, 0, :, a:b], sem)
        copy.start()
        copy.wait()

    operands = [blocks, here, there] + ([] if whole is None else [whole])
    return call(
        kernel,
        out_shape=jax.ShapeDtypeStruct(shape, here.dtype),
        in_specs=[ANY, VMEM, VMEM, ANY][: len(operands)],
        out_specs=ANY,
        input_output_aliases={} if whole is None else {3: 0},
        scratch_shapes=[pltpu.VMEM(here.shape, here.dtype)] + held(blocks),
        cost_estimate=cost(here.shape),
        name="finish",
    )(*operands)


def split(state, spans):
    def kernel(source, *refs):
        outs, sems = refs[:-1], refs[-1]
        copies = [
            pltpu.make_async_copy(source.at[:, a:b], out, sems.at[i])
            for i, ((a, b), out) in enumerate(zip(spans, outs))
        ]
        for copy in copies:
            copy.start()
        for copy in copies:
            copy.wait()

    return pl.pallas_call(
        kernel,
        out_shape=[jax.ShapeDtypeStruct((state.shape[0], b - a), state.dtype) for a, b in spans],
        compiler_params=pltpu.CompilerParams(vmem_limit_bytes=4 << 20),
        in_specs=[ANY],
        out_specs=[ANY] * len(spans),
        scratch_shapes=[pltpu.SemaphoreType.DMA((len(spans),))],
        cost_estimate=pl.CostEstimate(flops=1 << 36, bytes_accessed=1 << 26, transcendentals=0),
        name="split",
    )(state)


def spans_of(level, columns):
    begins = BEGINS[level]
    ends = begins[1:] + (8,)
    return {a: (a * columns // 8, b * columns // 8) for a, b in zip(begins, ends)}


def on_device(coefficients, transfer_blocks):
    state = coefficients[0, 0]
    columns = state.shape[1]
    levels = plan()
    spans = [spans_of(level, columns) for level in range(len(levels))]
    pieces = [dict() for _ in levels]
    pieces[0] = dict(zip(spans[0], split(state, list(spans[0].values()))))
    arrived = {}
    result = None
    for what, level, piece in ORDER:
        if what == "s":
            arrived[level, piece] = exchange(pieces[level][piece], *levels[level])
            continue
        here, there = pieces[level][piece], arrived[level, piece]
        first, last = spans[level][piece]
        if level == LAST:
            result = apply_in_place(
                level, transfer_blocks, here, there, result, (first, last), coefficients.shape
            )
            continue
        inner = {n: s for n, s in spans[level + 1].items() if first <= s[0] < last}
        within = [(a - first, b - first) for a, b in inner.values()]
        limit = 60 * 1024 * 1024 if (level, piece) in EARLY else 4 << 20
        sums = apply(level, transfer_blocks, here, there, within, limit)
        pieces[level + 1].update(zip(inner, sums))
    return result


def solution(mesh):
    in_specs = (P("gx", "gy", None, None), P(None, "gx", "gy", None, None))
    out_specs = P("gx", "gy", None, None)
    return jax.shard_map(
        on_device, mesh=mesh, in_specs=in_specs, out_specs=out_specs, check_vma=False
    )
```

```python
import functools

import jax
import jax.numpy as jnp
from jax import lax
from jax.experimental import pallas as pl
from jax.experimental.pallas import tpu as pltpu
from jax.sharding import PartitionSpec as P


BEGINS = ((0, 2, 4, 7), (0, 2, 4, 7), (0, 2, 4, 7), (0, 2, 4, 7))
ORDER = (
    ("s", 0, 0), ("s", 0, 2), ("s", 0, 4), ("d", 0, 0),
    ("s", 1, 0), ("s", 0, 7), ("d", 0, 2), ("s", 1, 2),
    ("d", 1, 0), ("s", 2, 0), ("d", 0, 4), ("s", 1, 4),
    ("d", 1, 2), ("s", 2, 2), ("d", 2, 0), ("s", 3, 0),
    ("d", 1, 4), ("s", 2, 4), ("d", 2, 2), ("s", 3, 2),
    ("d", 0, 7), ("s", 1, 7), ("d", 2, 4), ("s", 3, 4),
    ("d", 3, 0), ("d", 1, 7), ("s", 2, 7), ("d", 2, 7),
    ("s", 3, 7), ("d", 3, 2), ("d", 3, 4), ("d", 3, 7),
)
LAST = 3
EARLY = ()

ANY = pl.BlockSpec(memory_space=pl.ANY)
VMEM = pl.BlockSpec(memory_space=pltpu.VMEM)


def plan():
    high_top = lax.axis_size("gx").bit_length() - 2
    low_top = lax.axis_size("gy").bit_length() - 2
    return [("gx", high_top), ("gy", low_top), ("gx", high_top - 1), ("gy", low_top - 1)]


def exchange(block, axis, bit):
    route = [(i, i ^ (1 << bit)) for i in range(lax.axis_size(axis))]
    return lax.ppermute(block, axis, route)


def parts(value):
    high = value.astype(jnp.bfloat16)
    return high, (value - high.astype(jnp.float32)).astype(jnp.bfloat16)


def dot(left, right):
    single = functools.partial(jnp.dot, preferred_element_type=jnp.float32)
    left_high, left_low = parts(left)
    right_high, right_low = parts(right)
    return (single(left_low, right_high) + single(left_high, right_low)) + single(left_high, right_high)


def call(kernel, limit=4 << 20, **options):
    params = pltpu.CompilerParams(vmem_limit_bytes=limit)
    return pl.pallas_call(kernel, compiler_params=params, **options)


def cost(shape):
    rank, width = shape
    return pl.CostEstimate(
        flops=12 * rank * rank * width, bytes_accessed=12 * rank * width, transcendentals=0
    )


def products(level, blocks_ref, here, there):
    axis, bit = plan()[level]
    rank = here.shape[0]
    upper = jnp.bitwise_and(jnp.right_shift(lax.axis_index(axis), bit), 1)
    mine = blocks_ref[:, pl.ds(pl.multiple_of(upper * rank, rank), rank)]
    other = blocks_ref[:, pl.ds(pl.multiple_of((1 - upper) * rank, rank), rank)]
    return dot(mine, here) + dot(other, there)


def fetch(level, blocks_ref, held_ref, sem):
    copy = pltpu.make_async_copy(blocks_ref.at[level, 0, 0], held_ref, sem)
    copy.start()
    copy.wait()


def held(blocks):
    return [pltpu.VMEM(blocks.shape[3:], blocks.dtype), pltpu.SemaphoreType.DMA]


def apply(level, blocks, here, there, spans, limit):
    rank = here.shape[0]

    def kernel(blocks_ref, here_ref, there_ref, *refs):
        *outs, held_ref, sem = refs
        fetch(level, blocks_ref, held_ref, sem)
        for (a, b), out in zip(spans, outs):
            out[...] = products(level, held_ref, here_ref[:, a:b], there_ref[:, a:b])

    return call(
        kernel,
        out_shape=[jax.ShapeDtypeStruct((rank, b - a), here.dtype) for a, b in spans],
        in_specs=[ANY, VMEM, VMEM],
        out_specs=[VMEM] * len(spans),
        scratch_shapes=held(blocks),
        cost_estimate=cost(here.shape),
        limit=limit,
        name="apply",
    )(blocks, here, there)


def apply_in_place(level, blocks, here, there, whole, span, shape):
    a, b = span

    def kernel(blocks_ref, here_ref, there_ref, *refs):
        out_ref, sum_ref, held_ref, sem = refs[-4:]
        fetch(level, blocks_ref, held_ref, sem)
        sum_ref[...] = products(level, held_ref, here_ref[...], there_ref[...])
        copy = pltpu.make_async_copy(sum_ref, out_ref.at[0, 0, :, a:b], sem)
        copy.start()
        copy.wait()

    operands = [blocks, here, there] + ([] if whole is None else [whole])
    return call(
        kernel,
        out_shape=jax.ShapeDtypeStruct(shape, here.dtype),
        in_specs=[ANY, VMEM, VMEM, ANY][: len(operands)],
        out_specs=ANY,
        input_output_aliases={} if whole is None else {3: 0},
        scratch_shapes=[pltpu.VMEM(here.shape, here.dtype)] + held(blocks),
        cost_estimate=cost(here.shape),
        name="finish",
    )(*operands)


def split(state, spans):
    def kernel(source, *refs):
        outs, sems = refs[:-1], refs[-1]
        copies = [
            pltpu.make_async_copy(source.at[:, a:b], out, sems.at[i])
            for i, ((a, b), out) in enumerate(zip(spans, outs))
        ]
        for copy in copies:
            copy.start()
        for copy in copies:
            copy.wait()

    return pl.pallas_call(
        kernel,
        out_shape=[jax.ShapeDtypeStruct((state.shape[0], b - a), state.dtype) for a, b in spans],
        compiler_params=pltpu.CompilerParams(vmem_limit_bytes=4 << 20),
        in_specs=[ANY],
        out_specs=[ANY] * len(spans),
        scratch_shapes=[pltpu.SemaphoreType.DMA((len(spans),))],
        cost_estimate=pl.CostEstimate(flops=1 << 36, bytes_accessed=1 << 26, transcendentals=0),
        name="split",
    )(state)


def spans_of(level, columns):
    begins = BEGINS[level]
    ends = begins[1:] + (8,)
    return {a: (a * columns // 8, b * columns // 8) for a, b in zip(begins, ends)}


def on_device(coefficients, transfer_blocks):
    state = coefficients[0, 0]
    columns = state.shape[1]
    levels = plan()
    spans = [spans_of(level, columns) for level in range(len(levels))]
    pieces = [dict() for _ in levels]
    pieces[0] = dict(zip(spans[0], split(state, list(spans[0].values()))))
    arrived = {}
    result = None
    for what, level, piece in ORDER:
        if what == "s":
            arrived[level, piece] = exchange(pieces[level][piece], *levels[level])
            continue
        here, there = pieces[level][piece], arrived[level, piece]
        first, last = spans[level][piece]
        if level == LAST:
            result = apply_in_place(
                level, transfer_blocks, here, there, result, (first, last), coefficients.shape
            )
            continue
        inner = {n: s for n, s in spans[level + 1].items() if first <= s[0] < last}
        within = [(a - first, b - first) for a, b in inner.values()]
        limit = 60 * 1024 * 1024 if (level, piece) in EARLY else 4 << 20
        sums = apply(level, transfer_blocks, here, there, within, limit)
        pieces[level + 1].update(zip(inner, sums))
    return result


def solution(mesh):
    in_specs = (P("gx", "gy", None, None), P(None, "gx", "gy", None, None))
    out_specs = P("gx", "gy", None, None)
    return jax.shard_map(
        on_device, mesh=mesh, in_specs=in_specs, out_specs=out_specs, check_vma=False
    )
```

```python
import functools

import jax
import jax.numpy as jnp
from jax import lax
from jax.experimental import pallas as pl
from jax.experimental.pallas import tpu as pltpu
from jax.sharding import PartitionSpec as P


BEGINS = ((0, 2, 4, 7), (0, 2, 4, 7), (0, 2, 4, 7), (0, 2, 4, 7))
ORDER = (
    ("s", 0, 0), ("s", 0, 2), ("s", 0, 4), ("d", 0, 0),
    ("s", 1, 0), ("s", 0, 7), ("d", 0, 2), ("s", 1, 2),
    ("d", 1, 0), ("s", 2, 0), ("d", 1, 2), ("s", 2, 2),
    ("d", 0, 4), ("s", 1, 4), ("d", 2, 0), ("s", 3, 0),
    ("d", 1, 4), ("s", 2, 4), ("d", 2, 2), ("s", 3, 2),
    ("d", 0, 7), ("s", 1, 7), ("d", 2, 4), ("s", 3, 4),
    ("d", 3, 0), ("d", 1, 7), ("s", 2, 7), ("d", 2, 7),
    ("s", 3, 7), ("d", 3, 2), ("d", 3, 4), ("d", 3, 7),
)
LAST = 3
EARLY = ()

ANY = pl.BlockSpec(memory_space=pl.ANY)
VMEM = pl.BlockSpec(memory_space=pltpu.VMEM)


def plan():
    high_top = lax.axis_size("gx").bit_length() - 2
    low_top = lax.axis_size("gy").bit_length() - 2
    return [("gx", high_top), ("gy", low_top), ("gx", high_top - 1), ("gy", low_top - 1)]


def exchange(block, axis, bit):
    route = [(i, i ^ (1 << bit)) for i in range(lax.axis_size(axis))]
    return lax.ppermute(block, axis, route)


def parts(value):
    high = value.astype(jnp.bfloat16)
    return high, (value - high.astype(jnp.float32)).astype(jnp.bfloat16)


def dot(left, right):
    single = functools.partial(jnp.dot, preferred_element_type=jnp.float32)
    left_high, left_low = parts(left)
    right_high, right_low = parts(right)
    return (single(left_low, right_high) + single(left_high, right_low)) + single(left_high, right_high)


def call(kernel, limit=4 << 20, **options):
    params = pltpu.CompilerParams(vmem_limit_bytes=limit)
    return pl.pallas_call(kernel, compiler_params=params, **options)


def cost(shape):
    rank, width = shape
    return pl.CostEstimate(
        flops=12 * rank * rank * width, bytes_accessed=12 * rank * width, transcendentals=0
    )


def products(level, blocks_ref, here, there):
    axis, bit = plan()[level]
    rank = here.shape[0]
    upper = jnp.bitwise_and(jnp.right_shift(lax.axis_index(axis), bit), 1)
    mine = blocks_ref[level, 0, 0, :, pl.ds(pl.multiple_of(upper * rank, rank), rank)]
    other = blocks_ref[level, 0, 0, :, pl.ds(pl.multiple_of((1 - upper) * rank, rank), rank)]
    return dot(mine, here) + dot(other, there)


def apply(level, blocks, here, there, spans, limit):
    rank = here.shape[0]

    def kernel(blocks_ref, here_ref, there_ref, *refs):
        for (a, b), out in zip(spans, refs):
            out[...] = products(level, blocks_ref, here_ref[:, a:b], there_ref[:, a:b])

    return call(
        kernel,
        out_shape=[jax.ShapeDtypeStruct((rank, b - a), here.dtype) for a, b in spans],
        in_specs=[VMEM, VMEM, VMEM],
        out_specs=[VMEM] * len(spans),
        cost_estimate=cost(here.shape),
        limit=limit,
        name="apply",
    )(blocks, here, there)


def apply_in_place(level, blocks, here, there, whole, span, shape):
    a, b = span

    def kernel(blocks_ref, here_ref, there_ref, *refs):
        out_ref, sum_ref, sem = refs[-3:]
        sum_ref[...] = products(level, blocks_ref, here_ref[...], there_ref[...])
        copy = pltpu.make_async_copy(sum_ref, out_ref.at[0, 0, :, a:b], sem)
        copy.start()
        copy.wait()

    operands = [blocks, here, there] + ([] if whole is None else [whole])
    return call(
        kernel,
        out_shape=jax.ShapeDtypeStruct(shape, here.dtype),
        in_specs=[VMEM, VMEM, VMEM, ANY][: len(operands)],
        out_specs=ANY,
        input_output_aliases={} if whole is None else {3: 0},
        scratch_shapes=[pltpu.VMEM(here.shape, here.dtype), pltpu.SemaphoreType.DMA],
        cost_estimate=cost(here.shape),
        name="finish",
    )(*operands)


def split(state, spans):
    def kernel(source, *refs):
        outs, sems = refs[:-1], refs[-1]
        copies = [
            pltpu.make_async_copy(source.at[:, a:b], out, sems.at[i])
            for i, ((a, b), out) in enumerate(zip(spans, outs))
        ]
        for copy in copies:
            copy.start()
        for copy in copies:
            copy.wait()

    return pl.pallas_call(
        kernel,
        out_shape=[jax.ShapeDtypeStruct((state.shape[0], b - a), state.dtype) for a, b in spans],
        compiler_params=pltpu.CompilerParams(vmem_limit_bytes=4 << 20),
        in_specs=[ANY],
        out_specs=[ANY] * len(spans),
        scratch_shapes=[pltpu.SemaphoreType.DMA((len(spans),))],
        cost_estimate=pl.CostEstimate(flops=1 << 36, bytes_accessed=1 << 26, transcendentals=0),
        name="split",
    )(state)


def spans_of(level, columns):
    begins = BEGINS[level]
    ends = begins[1:] + (8,)
    return {a: (a * columns // 8, b * columns // 8) for a, b in zip(begins, ends)}


def on_device(coefficients, transfer_blocks):
    state = coefficients[0, 0]
    columns = state.shape[1]
    levels = plan()
    spans = [spans_of(level, columns) for level in range(len(levels))]
    pieces = [dict() for _ in levels]
    pieces[0] = dict(zip(spans[0], split(state, list(spans[0].values()))))
    arrived = {}
    result = None
    for what, level, piece in ORDER:
        if what == "s":
            arrived[level, piece] = exchange(pieces[level][piece], *levels[level])
            continue
        here, there = pieces[level][piece], arrived[level, piece]
        first, last = spans[level][piece]
        if level == LAST:
            result = apply_in_place(
                level, transfer_blocks, here, there, result, (first, last), coefficients.shape
            )
            continue
        inner = {n: s for n, s in spans[level + 1].items() if first <= s[0] < last}
        within = [(a - first, b - first) for a, b in inner.values()]
        limit = 60 * 1024 * 1024 if (level, piece) in EARLY else 4 << 20
        sums = apply(level, transfer_blocks, here, there, within, limit)
        pieces[level + 1].update(zip(inner, sums))
    return result


def solution(mesh):
    in_specs = (P("gx", "gy", None, None), P(None, "gx", "gy", None, None))
    out_specs = P("gx", "gy", None, None)
    return jax.shard_map(
        on_device, mesh=mesh, in_specs=in_specs, out_specs=out_specs, check_vma=False
    )
```
